32 devices in a mesh: row: 2 (over y), col: 4 (over x, core), chan: 4 (over z).
Axes of the slice: x: 2, y: 2, z: 4, core: 2. Of those that a mesh axis runs over, the one named last changes fastest.
Arguments:
- voltage: bfloat16 [2048, 96, 512], P(('row', 'col'), 'chan'), may hold values from -6 to 6
- channel_frequency_offset: float32 [96], P('chan'), may hold values from 0.7 to 1.3
- input_antenna_lookup: int32 [2048], replicated, may hold values from 0 to 2047, each once
- antenna_positions: float32 [2, 2048], replicated, may hold values from -400 to 400
- catalogue_direction: float32 [2, 512], replicated, may hold values from -0.01 to 0.01
- catalogue_flux: float32 [512], replicated, may hold values from 0.0005 to 0.005
- sky_source_index: int32 [4, 64], P('chan'), may hold values from 0 to 511
- baseline_tile_flagged: int32 [32, 32], replicated, may hold values 0 or 1
Outputs:
- visibility: bfloat16 [96, 2048, 4, 1024], P('chan', 'row', 'col')
- gain_solution: float32 [2, 2048, 96], P(None, ('row', 'col'), 'chan')
The draws below stay inside these ranges and needn't reach their ends.
Inputs may be any that keep to these rules, and one draw needn't show every extreme that they name: `input_antenna_lookup`: a permutation of 0 to 2047.
All inputs are finite; a program needn't handle non-finite values.
Results may differ from the reference program's by a relative error of at most 0.0033.
Values may be sent and summed in bfloat16 or wider, within the bound.
A program may use at most 384 MiB of HBM per device.

```python
import math
import jax
import jax.numpy as jnp
from jax import lax

INPUT_ANTENNAS = 2048
SAMPLES = 256
CH_DEV = 24
SOURCES = 64
CATALOG = 512
TILES = 32
ITERS = 3
CHANNELS = 96
GROUPS = 4
N_ROW = 2
N_COL = 4


def with_ends(drawn, stream_key, least, top_value):
    extent = drawn.shape
    spot = [jax.random.randint(jax.random.fold_in(stream_key, axis), (), 0, extent[axis]) for axis in range(len(extent))]
    drawn = drawn.at[tuple(spot)].set(least)
    longest = extent.index(max(extent))
    spot[longest] = (spot[longest] + 1) % extent[longest]
    return drawn.at[tuple(spot)].set(top_value)


def block_scale(stream_key, extent, pieces, least, high):
    factor_of = 1.0
    for axis_at, shards_of in pieces:
        heights = jax.random.uniform(jax.random.fold_in(jax.random.fold_in(stream_key, 6), axis_at), (shards_of,), jnp.float32, least / len(pieces), high / len(pieces))
        factor_of = factor_of * jnp.repeat(jnp.exp(heights), extent[axis_at] // shards_of).reshape((-1,) + (1,) * (len(extent) - 1 - axis_at))
    return factor_of


def normal_values(stream_key, extent, spread, reach, pieces=(), kind=jnp.bfloat16):
    values = spread * jax.random.normal(stream_key, extent, jnp.float32)
    if pieces:
        values = values * block_scale(stream_key, extent, pieces, -0.22, 0.18)
    return jnp.clip(values, -reach, reach).astype(kind)


def setup_inputs(seed: int = 0) -> dict:
    arg_keys = jax.random.split(jax.random.key(seed), 9)
    return {
        "voltage": normal_values(arg_keys[0], (INPUT_ANTENNAS, CHANNELS, 2 * SAMPLES), 1.0, 6.0, ((0, 8), (1, 4))),
        "channel_frequency_offset": jnp.clip(0.7 + 0.59999996 * jax.random.uniform(arg_keys[1], (CHANNELS,), jnp.float32) ** block_scale(arg_keys[1], (CHANNELS,), ((0, 4),), -0.2, 0.2), 0.7, 1.3),
        "input_antenna_lookup": jax.random.permutation(arg_keys[2], INPUT_ANTENNAS).astype(jnp.int32),
        "antenna_positions": jnp.clip(jax.random.uniform(arg_keys[3], (2, INPUT_ANTENNAS), jnp.float32, -400.0, 400.0), -400.0, 400.0),
        "catalogue_direction": jnp.clip(jax.random.uniform(arg_keys[4], (2, CATALOG), jnp.float32, -0.01, 0.01), -0.01, 0.01),
        "catalogue_flux": jnp.clip(jnp.exp(jax.random.uniform(arg_keys[5], (CATALOG,), jnp.float32, math.log(0.0005), math.log(0.005))), 0.0005, 0.005),
        "sky_source_index": with_ends(jax.random.randint(arg_keys[6], (GROUPS, SOURCES), 0, CATALOG), jax.random.fold_in(arg_keys[6], 1), 0, CATALOG - 1).astype(jnp.int32),
        "baseline_tile_flagged": with_ends((jax.random.randint(arg_keys[7], (TILES, TILES), 0, 8) < 1).astype(jnp.int32), jax.random.fold_in(arg_keys[7], 1), 0, 1),
    }


def reference(voltage, channel_frequency_offset, input_antenna_lookup, antenna_positions, catalogue_direction, catalogue_flux, sky_source_index, baseline_tile_flagged):
    highest = lax.Precision.HIGHEST
    row_block = INPUT_ANTENNAS // N_ROW
    col_block = INPUT_ANTENNAS // N_COL
    sub_block = INPUT_ANTENNAS // (N_ROW * N_COL)
    slots = jnp.arange(INPUT_ANTENNAS, dtype=jnp.int32)
    within = slots % col_block
    col_order = (within // sub_block) * row_block + (slots // col_block) * sub_block + within % sub_block
    tiles = slots // (INPUT_ANTENNAS // TILES)
    flagged = baseline_tile_flagged[tiles][:, tiles]
    weight = 1.0 - jnp.maximum(flagged, flagged.T).astype(jnp.float32)
    eastward_position = antenna_positions[0][input_antenna_lookup]
    northward_position = antenna_positions[1][input_antenna_lookup]

    def per_channel(index):
        chan_volt = lax.dynamic_index_in_dim(voltage, index, 1, keepdims=False).astype(jnp.float32)
        real_part = chan_volt[:, :SAMPLES]
        imag_part = chan_volt[:, SAMPLES:]
        vis_re = (jnp.dot(real_part, real_part.T, precision=highest) + jnp.dot(imag_part, imag_part.T, precision=highest)) / SAMPLES
        vis_im = (jnp.dot(imag_part, real_part.T, precision=highest) - jnp.dot(real_part, imag_part.T, precision=highest)) / SAMPLES
        group = index // CH_DEV
        source_ids = lax.dynamic_index_in_dim(sky_source_index, group, 0, keepdims=False)
        source_cosine_l = catalogue_direction[0][source_ids]
        source_cosine_m = catalogue_direction[1][source_ids]
        flux = catalogue_flux[source_ids]
        freq = lax.dynamic_index_in_dim(channel_frequency_offset, index, 0, keepdims=False)
        phase = (-2.0 * math.pi * freq) * (eastward_position[:, None] * source_cosine_l[None, :] + northward_position[:, None] * source_cosine_m[None, :])
        steer_re = jnp.cos(phase)
        steer_im = jnp.sin(phase)
        model_re = jnp.dot(steer_re * flux, steer_re.T, precision=highest) + jnp.dot(steer_im * flux, steer_im.T, precision=highest)
        model_im = jnp.dot(steer_im * flux, steer_re.T, precision=highest) - jnp.dot(steer_re * flux, steer_im.T, precision=highest)
        gain_re = jnp.ones((INPUT_ANTENNAS,), jnp.float32)
        gain_im = jnp.zeros((INPUT_ANTENNAS,), jnp.float32)
        for iteration in range(ITERS):
            z_re = gain_re[:, None] * model_re - gain_im[:, None] * model_im
            z_im = gain_re[:, None] * model_im + gain_im[:, None] * model_re
            num_re = jnp.sum(weight * (vis_re * z_re + vis_im * z_im), axis=0)
            num_im = jnp.sum(weight * (vis_re * z_im - vis_im * z_re), axis=0)
            denom = jnp.sum(weight * (z_re * z_re + z_im * z_im), axis=0) + 1e-6
            gain_re = (gain_re + num_re / denom) * 0.5
            gain_im = (gain_im + num_im / denom) * 0.5
        ordered_re = vis_re[:, col_order].reshape(INPUT_ANTENNAS, N_COL, col_block)
        ordered_im = vis_im[:, col_order].reshape(INPUT_ANTENNAS, N_COL, col_block)
        visible = jnp.concatenate([ordered_re, ordered_im], axis=2).astype(jnp.bfloat16)
        return visible, jnp.stack([gain_re, gain_im])

    visibility, gain_all = lax.map(per_channel, jnp.arange(CHANNELS, dtype=jnp.int32))
    gain_solution = jnp.transpose(gain_all, (1, 2, 0))
    return visibility, gain_solution
```

```python
import functools
import math

import jax
import jax.numpy as jnp
import numpy as np
from jax import lax
from jax.experimental import pallas as pl
from jax.experimental.pallas import tpu as pltpu
from jax.sharding import PartitionSpec as P

ITERS = 3
CHUNKS = 4
PARTS = (4, 5, 5, 5, 3, 2)
AHEAD = 2
HELD, RING = 15, 3
STRIP = 128
MESH = pl.DeviceIdType.MESH


def cosine_coefficients(degree=8):
    nodes = np.cos(np.pi * (np.arange(400) + 0.5) / 400)
    y = 0.125 * (nodes + 1.0)
    fit = np.polynomial.chebyshev.Chebyshev.fit(
        y, np.cos(2.0 * np.pi * np.sqrt(y)), degree, domain=[0.0, 0.25]
    )
    return [float(c) for c in fit.convert(kind=np.polynomial.Polynomial).coef]


COS_COEF = cosine_coefficients()


def cos_turns(turns):
    r = turns - jnp.round(turns)
    y = r * r
    acc = jnp.full_like(y, COS_COEF[-1])
    for c in COS_COEF[-2::-1]:
        acc = acc * y + c
    return acc


def split(x):
    hi = x.astype(jnp.bfloat16)
    lo = (x - hi.astype(jnp.float32)).astype(jnp.bfloat16)
    return hi, lo


def column_sum(x):
    return jnp.sum(x, axis=0, keepdims=True)


NT = (((1,), (1,)), ((), ()))


def correlate_kernel(base, tile, n_rows, n_cols, freq_ref, place_ref, wt_ref, rbase_ref, cbase_ref, lane_ref,
                     *rest):
    rows_refs, cols_refs = rest[:n_rows], rest[n_rows:n_rows + n_cols]
    vis_ref, cre_ref, cim_ref, den_ref, sum_ref, rows_ref, part_ref, steer_ref = rest[-8:]
    samples = rows_ref.shape[1] // 2
    row_block = rows_ref.shape[0]
    col_block = part_ref.shape[0] // 2
    half = lane_ref.shape[1] // 2
    lanes = 2 * half
    freq = freq_ref[base + pl.program_id(0)]
    for j, ref in enumerate(rows_refs):
        size = ref.shape[1]
        at = pl.ds(pl.multiple_of(place_ref[j] * size, size), size) if n_rows > 1 else pl.ds(0, size)
        rows_ref[at, :] = ref[0]
    for j, ref in enumerate(cols_refs):
        size = ref.shape[1]
        start = pl.multiple_of(place_ref[n_rows + j] * size, size) if n_cols > 1 else 0
        scaled = ref[0] * jnp.bfloat16(1.0 / samples)
        part_ref[pl.ds(start, size), :] = scaled
        part_ref[pl.ds(col_block + start, size), :samples] = -scaled[:, samples:]
        part_ref[pl.ds(col_block + start, size), samples:] = scaled[:, :samples]
    offset = lane_ref[0:1, :]
    flux = lane_ref[1:2, :]
    sign = lane_ref[2:3, :]
    col_steer = cos_turns(cbase_ref[...] * freq + offset)
    swapped = pltpu.roll(col_steer, half, 1) * sign
    for j, s in enumerate((col_steer, swapped)):
        hi, lo = split(s)
        at = pl.ds(j * col_block, col_block)
        steer_ref[at, :lanes] = hi
        steer_ref[at, lanes:2 * lanes] = hi
        steer_ref[at, 2 * lanes:] = lo

    def step(i, sums):
        at = pl.ds(pl.multiple_of(i * tile, tile), tile)
        v = lax.dot_general(rows_ref[at, :], part_ref[...], NT, preferred_element_type=jnp.float32)
        vis_ref[0, at, :] = v.astype(jnp.bfloat16)
        hi, lo = split(cos_turns(rbase_ref[at, :] * freq + offset) * flux)
        m = lax.dot_general(
            jnp.concatenate([hi, lo, hi], axis=1), steer_ref[...], NT, preferred_element_type=jnp.float32
        )
        w = wt_ref[at, :]
        vr, vi = v[:, :col_block], v[:, col_block:]
        mr, mi = m[:, :col_block] * w, m[:, col_block:] * w
        cre = vr * mr + vi * mi
        cim = vr * mi - vi * mr
        den = mr * mr + mi * mi
        cre_ref[0, at, :] = cre.astype(jnp.bfloat16)
        cim_ref[0, at, :] = cim.astype(jnp.bfloat16)
        den_ref[0, at, :] = den.astype(jnp.bfloat16)
        return tuple(s + column_sum(x) for s, x in zip(sums, (cre, cim, den)))

    zero = jnp.zeros((1, col_block), jnp.float32)
    sums = lax.fori_loop(0, row_block // tile, step, (zero, zero, zero))
    for j in range(3):
        sum_ref[0, j:j + 1, :] = sums[j]


def correlate(base, freq, place, rows, cols, weight, rbase, cbase, lane_rows, channels, earlier):
    chans, _, width = rows[0].shape
    row_block, col_block = weight.shape
    lanes = lane_rows.shape[1]
    tile = min(256, row_block)

    def whole(a):
        return pl.BlockSpec(a.shape, lambda k: (0,) * a.ndim)

    def slab(*shape):
        return pl.BlockSpec((1,) + shape, lambda k: (k, 0, 0))

    in_specs = [
        pl.BlockSpec(memory_space=pltpu.SMEM),
        pl.BlockSpec(memory_space=pltpu.SMEM),
        whole(weight),
        whole(rbase),
        whole(cbase),
        whole(lane_rows),
    ] + [slab(a.shape[1], width) for a in rows + cols]
    args = [freq, place, weight, rbase, cbase, lane_rows] + rows + cols
    aliases = {}
    if earlier is not None:
        in_specs.append(pl.BlockSpec(memory_space=pl.ANY))
        args.append(earlier)
        aliases = {len(args) - 1: 0}
    stored = jax.ShapeDtypeStruct((chans, row_block, col_block), jnp.bfloat16)
    flops = chans * row_block * 2 * col_block * (2 * width + 6 * lanes)
    return pl.pallas_call(
        functools.partial(correlate_kernel, base, tile, len(rows), len(cols)),
        grid=(chans,),
        in_specs=in_specs,
        out_specs=[
            pl.BlockSpec((1, row_block, 2 * col_block), lambda k: (k + base, 0, 0)),
            slab(row_block, col_block),
            slab(row_block, col_block),
            slab(row_block, col_block),
            slab(3, col_block),
        ],
        out_shape=[
            jax.ShapeDtypeStruct((channels, row_block, 2 * col_block), jnp.bfloat16),
            stored,
            stored,
            stored,
            jax.ShapeDtypeStruct((chans, 3, col_block), jnp.float32),
        ],
        scratch_shapes=[
            pltpu.VMEM((row_block, width), jnp.bfloat16),
            pltpu.VMEM((2 * col_block, width), jnp.bfloat16),
            pltpu.VMEM((2 * col_block, 3 * lanes), jnp.bfloat16),
        ],
        input_output_aliases=aliases,
        compiler_params=pltpu.CompilerParams(vmem_limit_bytes=60 * 2**20),
        cost_estimate=pl.CostEstimate(
            flops=flops, bytes_accessed=chans * row_block * col_block * 14, transcendentals=0
        ),
        name="correlate",
    )(*args)


def gain_kernel(tile, gain_ref, cre_ref, cim_ref, den_ref, sum_ref):
    row_block, col_block = cre_ref.shape[1:]
    total = [jnp.zeros((1, col_block), jnp.float32) for _ in range(3)]
    for i in range(row_block // tile):
        at = pl.ds(i * tile, tile)
        g = jnp.transpose(gain_ref[0, :, i * tile:(i + 1) * tile])
        gr, gi, power = g[:, 0:1], g[:, 1:2], g[:, 2:3]
        cre = cre_ref[0, at, :].astype(jnp.float32)
        cim = cim_ref[0, at, :].astype(jnp.float32)
        den = den_ref[0, at, :].astype(jnp.float32)
        total[0] += column_sum(gr * cre - gi * cim)
        total[1] += column_sum(gr * cim + gi * cre)
        total[2] += column_sum(power * den)
    for j in range(3):
        sum_ref[0, j:j + 1, :] = total[j]


def gain_sums(gain_re, gain_im, cre, cim, den):
    chans, row_block, col_block = cre.shape
    power = gain_re * gain_re + gain_im * gain_im
    gains = jnp.stack([gain_re, gain_im, power] + [jnp.zeros_like(power)] * 5, axis=1)

    def slab(*shape):
        return pl.BlockSpec((1,) + shape, lambda k: (k, 0, 0))

    return pl.pallas_call(
        functools.partial(gain_kernel, min(128, row_block)),
        grid=(chans,),
        in_specs=[slab(8, row_block)] + [slab(row_block, col_block)] * 3,
        out_specs=slab(3, col_block),
        out_shape=jax.ShapeDtypeStruct((chans, 3, col_block), jnp.float32),
        compiler_params=pltpu.CompilerParams(vmem_limit_bytes=60 * 2**20),
        cost_estimate=pl.CostEstimate(
            flops=chans * row_block * col_block * 10,
            bytes_accessed=chans * row_block * col_block * 6,
            transcendentals=0,
        ),
        name="gain_sums",
    )(gains, cre, cim, den)


def swap(x, axis):
    return lax.ppermute(x, axis, [(0, 1), (1, 0)])


def column_blocks(x, n_row):
    if n_row != 2:
        return [jnp.transpose(lax.all_gather(jnp.transpose(x, (1, 0, 2)), "row", axis=0, tiled=True), (1, 0, 2))]
    return [x, swap(x, "row")]


def row_blocks(x, n_col):
    if n_col != 4:
        return [jnp.transpose(lax.all_gather(jnp.transpose(x, (1, 0, 2)), "col", axis=0, tiled=True), (1, 0, 2))]
    far = lax.ppermute(x, "col", [(c, c ^ 2) for c in range(n_col)])
    mate = [(c, c ^ 1) for c in range(n_col)]
    return [x, lax.ppermute(x, "col", mate), far, lax.ppermute(far, "col", mate)]


def own_sums(part, row_id, n_row, sub_block):
    if n_row != 2:
        part = lax.psum(part, "row")
        return lax.dynamic_slice_in_dim(part, row_id * sub_block, sub_block, 2)
    mine = lax.dynamic_slice_in_dim(part, row_id * sub_block, sub_block, 2)
    theirs = lax.dynamic_slice_in_dim(part, (1 - row_id) * sub_block, sub_block, 2)
    return mine + swap(theirs, "row")


def gather_gains(own, col_id, n_col, sub_block):
    if n_col != 4:
        return lax.all_gather(own, "col", axis=2, tiled=True)
    blocks = [own] + [
        lax.ppermute(own, "col", [((c + j) % n_col, c) for c in range(n_col)]) for j in range(1, n_col)
    ]
    twice = jnp.concatenate(blocks + blocks, axis=2)
    return lax.dynamic_slice_in_dim(twice, (n_col - col_id) % n_col * sub_block, n_col * sub_block, 2)


def fused_kernel(base, n_rows, n_cols, freq_ref, place_ref, wt_ref, rbase_ref, cbase_ref, lane_ref, *rest):
    rows_refs, cols_refs = rest[:n_rows], rest[n_rows:n_rows + n_cols]
    vis_ref, cre_ref, cim_ref, den_ref, sum_ref, rows_ref, part_ref, rst_ref, cst_ref = rest[-9:]
    samples = rows_ref.shape[1] // 2
    col_block = part_ref.shape[0] // 2
    half = lane_ref.shape[1] // 2
    lanes = 2 * half
    width = STRIP
    freq = freq_ref[base + pl.program_id(0)]
    for j, ref in enumerate(rows_refs):
        size = ref.shape[1]
        rows_ref[pl.ds(pl.multiple_of(place_ref[j] * size, size), size), :] = ref[0]
    for j, ref in enumerate(cols_refs):
        size = ref.shape[1]
        start = pl.multiple_of(place_ref[n_rows + j] * 2 * size, 2 * size)
        for u in range(size // width):
            scaled = ref[0, u * width:(u + 1) * width, :] * jnp.bfloat16(1.0 / samples)
            at = start + 2 * u * width
            part_ref[pl.ds(at, width), :] = scaled
            part_ref[pl.ds(at + width, width), :samples] = -scaled[:, samples:]
            part_ref[pl.ds(at + width, width), samples:] = scaled[:, :samples]
    offset, flux, sign = lane_ref[0:1, :], lane_ref[1:2, :], lane_ref[2:3, :]
    col_steer = cos_turns(cbase_ref[...] * freq + offset)
    swapped = pltpu.roll(col_steer, half, 1) * sign
    for j, s in enumerate((col_steer, swapped)):
        hi, lo = split(s)
        for u in range(col_block // width):
            at = pl.ds((2 * u + j) * width, width)
            cst_ref[at, :lanes] = hi[u * width:(u + 1) * width]
            cst_ref[at, lanes:] = lo[u * width:(u + 1) * width]
    row_steer = (cos_turns(rbase_ref[...] * freq + offset) * flux).astype(jnp.bfloat16)
    rst_ref[:, :lanes] = row_steer
    rst_ref[:, lanes:] = row_steer
    for u in range(col_block // width):
        strip = slice(2 * u * width, 2 * (u + 1) * width)
        at = slice(u * width, (u + 1) * width)
        v = lax.dot_general(rows_ref[...], part_ref[strip, :], NT, preferred_element_type=jnp.float32)
        m = lax.dot_general(rst_ref[...], cst_ref[strip, :], NT, preferred_element_type=jnp.float32)
        w = wt_ref[:, at]
        vr, vi = v[:, :width], v[:, width:]
        mr, mi = m[:, :width] * w, m[:, width:] * w
        vis_ref[0, :, at] = vr.astype(jnp.bfloat16)
        vis_ref[0, :, col_block + u * width:col_block + (u + 1) * width] = vi.astype(jnp.bfloat16)
        cre = vr * mr + vi * mi
        cim = vr * mi - vi * mr
        den = mr * mr + mi * mi
        for j, (ref, x) in enumerate(((cre_ref, cre), (cim_ref, cim), (den_ref, den))):
            ref[0, :, at] = x.astype(jnp.bfloat16)
            sum_ref[0, j:j + 1, at] = column_sum(x)


def fused(base, freq, place, rows, cols, weight, rbase, cbase, lane_rows, channels, earlier):
    chans, size, width = rows[2].shape
    row_block, col_block = weight.shape
    lanes = lane_rows.shape[1]

    def whole(a):
        return pl.BlockSpec(a.shape, lambda k: (0,) * a.ndim)

    def slab(*shape):
        return pl.BlockSpec((1,) + shape, lambda k: (k, 0, 0))

    def placed(*shape):
        return pl.BlockSpec((1,) + shape, lambda k: (k + base, 0, 0))

    def block(a):
        return slab(size, width) if a.shape[0] == chans else placed(size, width)

    tables = [weight, rbase, cbase, lane_rows]
    in_specs = [pl.BlockSpec(memory_space=pltpu.SMEM)] * 2 + [whole(a) for a in tables]
    in_specs += [block(a) for a in rows + cols]
    args = [freq, place] + tables + rows + cols
    aliases = {}
    for j, array in enumerate(earlier or ()):
        in_specs.append(pl.BlockSpec(memory_space=pl.ANY))
        aliases[len(args)] = j
        args.append(array)
    stored = jax.ShapeDtypeStruct((channels, row_block, col_block), jnp.bfloat16)
    return pl.pallas_call(
        functools.partial(fused_kernel, base, len(rows), len(cols)),
        grid=(chans,),
        in_specs=in_specs,
        out_specs=[placed(row_block, 2 * col_block)] + [placed(row_block, col_block)] * 3 + [placed(3, col_block)],
        out_shape=[jax.ShapeDtypeStruct((channels, row_block, 2 * col_block), jnp.bfloat16)]
        + [stored] * 3
        + [jax.ShapeDtypeStruct((channels, 3, col_block), jnp.float32)],
        scratch_shapes=[
            pltpu.VMEM((row_block, width), jnp.bfloat16),
            pltpu.VMEM((2 * col_block, width), jnp.bfloat16),
            pltpu.VMEM((row_block, 2 * lanes), jnp.bfloat16),
            pltpu.VMEM((2 * col_block, 2 * lanes), jnp.bfloat16),
        ],
        input_output_aliases=aliases,
        compiler_params=pltpu.CompilerParams(vmem_limit_bytes=62 * 2**20),
        cost_estimate=pl.CostEstimate(flops=1, bytes_accessed=1, transcendentals=0),
        name="correlate_fused",
    )(*args)


def calibrate_kernel(counts, held_count, ring, sums_ref, cre_hbm, cim_hbm, den_hbm, out_ref, cre, cim, den, lhs,
                     part_a, part_b, landed_a, landed_b, gain_a, gain_b, load_sem, send_sem, recv_sem):
    held = (cre, cim, den)
    parts, landings, gains = (part_a, part_b), (landed_a, landed_b), (gain_a, gain_b)
    firsts = (0, counts[0])
    total = sum(counts)
    turning = total - held_count
    sub = part_a.shape[3]
    r, c = lax.axis_index("row"), lax.axis_index("col")
    cols = [c, c + 1 - 2 * (c % 2), (c + 2) % 4, 3 - c]
    peers = [(d, j) for d in range(2) for j in range(4) if d or j]
    spots = {(d, j): ((1 - r) if d else r, cols[j]) for d, j in peers}
    barrier = pltpu.get_barrier_semaphore()
    for peer in peers:
        row, col = spots[peer]
        pl.semaphore_signal(barrier, inc=1, device_id={"row": row, "col": col}, device_id_type=MESH)

    def loads(k, slot):
        return [
            pltpu.make_async_copy(src.at[k], dst.at[slot], load_sem.at[slot, j])
            for j, (src, dst) in enumerate(zip((cre_hbm, cim_hbm, den_hbm), held))
        ]

    def fetch(k, carry):
        for copy in loads(k, k):
            copy.start()
        return carry

    lax.fori_loop(0, held_count + ring, fetch, 0)
    lhs[...] = jnp.zeros_like(lhs)
    for part, first, count in zip(parts, firsts, counts):
        for j in range(3):
            for h in range(2):
                for k in range(count):
                    part[h, j, k:k + 1, :] = sums_ref[first + k, j:j + 1, h * sub:(h + 1) * sub]

    def fits(k, slot, part, at):
        matrix = lhs[k].astype(jnp.bfloat16)
        a, b, d = (jnp.dot(matrix, m[slot], preferred_element_type=jnp.float32) for m in held)
        rows = (
            a[0:1] + a[1:2] - b[2:3] - b[3:4],
            b[0:1] + b[1:2] + a[2:3] + a[3:4],
            d[4:5] + d[5:6],
        )
        for j, row in enumerate(rows):
            for h in range(2):
                part[h, j, pl.ds(at, 1), :] = row[:, h * sub:(h + 1) * sub]

    def refit(side, iteration):
        first, last = firsts[side], firsts[side] + counts[side]

        def resident(k, carry):
            if iteration == 1:
                for copy in loads(k, k):
                    copy.wait()
            fits(k, k, parts[side], k - first)
            return carry

        def turned(k, carry):
            slot = held_count + (k - held_count) % ring
            for copy in loads(k, slot):
                copy.wait()
            fits(k, slot, parts[side], k - first)
            following = held_count + (k - held_count + ring) % turning

            def start():
                for copy in loads(following, slot):
                    copy.start()

            if iteration == 1:
                start()
            else:
                pl.when(k + ring < total)(start)
            return carry

        split_at = min(max(held_count, first), last)
        if first < split_at:
            lax.fori_loop(first, split_at, resident, 0)
        if split_at < last:
            lax.fori_loop(split_at, last, turned, 0)

    def send(side, iteration):
        part, landed = parts[side], landings[side]
        copies = []
        for d, j in [(1, 0)] if iteration + 1 == ITERS else peers:
            row, col = spots[d, j]
            copies.append(
                pltpu.make_async_remote_copy(
                    src_ref=part.at[row],
                    dst_ref=landed.at[iteration, r, c],
                    send_sem=send_sem.at[side, iteration, 4 * d + j],
                    recv_sem=recv_sem.at[side, iteration, 4 * d + j],
                    device_id={"row": row, "col": col},
                    device_id_type=MESH,
                )
            )
        for copy in copies:
            copy.start()
        landed[iteration, r, c] = part[r]
        return copies

    def update(side, iteration, block):
        sums = landings[side][iteration, 0, block] + landings[side][iteration, 1, block]
        total = sums[2] + 1e-06
        if iteration:
            re, im = gains[side][block, 0], gains[side][block, 1]
        else:
            re, im = jnp.ones_like(total), jnp.zeros_like(total)
        return (re + sums[0] / total) * 0.5, (im + sums[1] / total) * 0.5

    def advance(side, iteration):
        for b in range(4):
            re, im = update(side, iteration, b)
            gains[side][b, 0], gains[side][b, 1] = re, im
            rows = []
            for x in (re, im, re * re + im * im):
                hi = x.astype(jnp.bfloat16).astype(jnp.float32)
                rows += [hi, x - hi]
            for k in range(counts[side]):
                for j, x in enumerate(rows):
                    lhs[firsts[side] + k, j:j + 1, b * sub:(b + 1) * sub] = x[k:k + 1]

    pl.semaphore_wait(barrier, len(peers))
    pending = [send(side, 0) for side in range(2)]
    for iteration in range(1, ITERS):
        for side in range(2):
            for copy in pending[side]:
                copy.wait()
            advance(side, iteration - 1)
            refit(side, iteration)
            pending[side] = send(side, iteration)
    for side in range(2):
        for copy in pending[side]:
            copy.wait()
        re, im = update(side, ITERS - 1, c)
        at = slice(firsts[side], firsts[side] + counts[side])
        out_ref[0, at, :], out_ref[1, at, :] = re, im


def calibrate(stored, sums):
    chans, row_block, col_block = stored[0].shape
    counts = (chans // 2, chans - chans // 2)
    sub = col_block // 2
    held = pltpu.VMEM((HELD + RING, row_block, col_block), jnp.bfloat16)
    in_vmem = pl.BlockSpec(memory_space=pltpu.VMEM)
    return pl.pallas_call(
        functools.partial(calibrate_kernel, counts, HELD, RING),
        in_specs=[in_vmem] + [pl.BlockSpec(memory_space=pl.ANY)] * 3,
        out_specs=in_vmem,
        out_shape=jax.ShapeDtypeStruct((2, chans, sub), jnp.float32),
        scratch_shapes=[held, held, held, pltpu.VMEM((chans, 16, row_block), jnp.float32)]
        + [pltpu.VMEM((2, 3, n, sub), jnp.float32) for n in counts]
        + [pltpu.VMEM((ITERS, 2, 4, 3, n, sub), jnp.float32) for n in counts]
        + [pltpu.VMEM((4, 2, n, sub), jnp.float32) for n in counts]
        + [
            pltpu.SemaphoreType.DMA((HELD + RING, 3)),
            pltpu.SemaphoreType.DMA((2, ITERS, 8)),
            pltpu.SemaphoreType.DMA((2, ITERS, 8)),
        ],
        compiler_params=pltpu.CompilerParams(
            collective_id=0, has_side_effects=True, vmem_limit_bytes=62 * 2**20
        ),
        cost_estimate=pl.CostEstimate(
            flops=chans * row_block * col_block * 40,
            bytes_accessed=chans * row_block * col_block * 8,
            transcendentals=0,
        ),
        name="calibrate",
    )(sums, *stored)


def body(
    voltage,
    channel_frequency_offset,
    input_antenna_lookup,
    antenna_positions,
    catalogue_direction,
    catalogue_flux,
    sky_source_index,
    baseline_tile_flagged,
):
    highest = lax.Precision.HIGHEST
    n_row = lax.axis_size("row")
    n_col = lax.axis_size("col")
    sub_block, channels, width = voltage.shape
    row_block = sub_block * n_col
    col_block = sub_block * n_row
    total = row_block * n_row
    row_id = lax.axis_index("row")
    col_id = lax.axis_index("col")

    chunk = channels // CHUNKS if channels % CHUNKS == 0 else channels
    spots = [col_id ^ j for j in range(4)] if n_col == 4 else [0 * col_id]
    spots += [row_id, 1 - row_id] if n_row == 2 else [0 * row_id]
    place = jnp.stack(spots).astype(jnp.int32)

    row_ids = row_id * row_block + jnp.arange(row_block, dtype=jnp.int32)
    slots = jnp.arange(col_block, dtype=jnp.int32)
    col_ids = slots // sub_block * row_block + col_id * sub_block + slots % sub_block
    tiles = baseline_tile_flagged.shape[0]
    tile_width = total // tiles
    kept = 1.0 - jnp.maximum(baseline_tile_flagged, baseline_tile_flagged.T).astype(jnp.float32)
    tile_ids = jnp.arange(tiles, dtype=jnp.int32)
    row_pick = (row_ids[:, None] // tile_width == tile_ids).astype(jnp.float32)
    col_pick = (col_ids[:, None] // tile_width == tile_ids).astype(jnp.float32)
    weight = jnp.dot(jnp.dot(row_pick, kept), col_pick.T)

    row_antennas = lax.dynamic_slice_in_dim(input_antenna_lookup, row_id * row_block, row_block)
    col_antennas = lax.dynamic_slice_in_dim(
        input_antenna_lookup.reshape(n_row, n_col, sub_block), col_id, 1, 1
    ).reshape(col_block)
    antennas = jnp.concatenate([row_antennas, col_antennas])
    picked = (antennas[:, None] == jnp.arange(total, dtype=jnp.int32)).astype(jnp.float32)
    where = jnp.dot(picked, antenna_positions.T, precision=highest)
    sources = sky_source_index[0]
    catalogue = jnp.concatenate([catalogue_direction, catalogue_flux[None]], axis=0)
    chosen = (sources[:, None] == jnp.arange(catalogue.shape[1], dtype=jnp.int32)).astype(jnp.float32)
    sky = lax.dot_general(catalogue, chosen, (((1,), (1,)), ((), ())), precision=highest)
    twice = jnp.concatenate([sky, sky], axis=1)
    turns = where[:, 0:1] * twice[0:1] + where[:, 1:2] * twice[1:2]
    n_src = sources.shape[0]
    ones = jnp.ones((n_src,), jnp.float32)
    lane_rows = jnp.stack(
        [jnp.concatenate([0.0 * ones, 0.25 * ones]), twice[2], jnp.concatenate([-ones, ones])]
        + [jnp.zeros((2 * n_src,), jnp.float32)] * 5
    )

    if n_row == 2 and n_col == 4 and channels == sum(PARTS) and sub_block % STRIP == 0 and 2 * n_src == 128:
        return pipelined(voltage, channel_frequency_offset, place, weight, turns, lane_rows)

    visible = None
    finals = []
    done = []
    for base in range(0, channels, chunk):
        piece = jnp.transpose(voltage[:, base:base + chunk, :], (1, 0, 2))
        if len(done) >= 2:
            piece, done[-2][3] = lax.optimization_barrier((piece, done[-2][3]))
        rows, cols = row_blocks(piece, n_col), column_blocks(piece, n_row)
        visible, *kept_sums = correlate(
            base, channel_frequency_offset, place, rows, cols, weight,
            turns[:row_block], turns[row_block:], lane_rows, channels, visible,
        )
        done.append(kept_sums)
    for cre, cim, den, part in done:
        own = None
        for iteration in range(ITERS):
            if iteration:
                gains = gather_gains(own, col_id, n_col, sub_block)
                part = gain_sums(gains[:, 0], gains[:, 1], cre, cim, den)
            sums = own_sums(part, row_id, n_row, sub_block)
            if own is None:
                own = jnp.concatenate([jnp.ones_like(sums[:, :1]), jnp.zeros_like(sums[:, :1])], axis=1)
            own = (own + sums[:, :2] / (sums[:, 2:3] + 1e-06)) * 0.5
        finals.append(own)
    gain_solution = jnp.transpose(jnp.concatenate(finals, axis=0), (1, 2, 0))
    return (visible.reshape(channels, row_block, 1, 2 * col_block), gain_solution)


def pipelined(voltage, freq, place, weight, turns, lane_rows):
    sub_block, channels, width = voltage.shape
    row_block, col_block = weight.shape
    mate = [(c, c ^ 1) for c in range(4)]
    bases = [sum(PARTS[:i]) for i in range(len(PARTS))]
    pieces = [jnp.transpose(voltage[:, b:b + n, :], (1, 0, 2)) for b, n in zip(bases, PARTS)]

    def send(piece):
        return lax.ppermute(piece, "col", [(c, c ^ 2) for c in range(4)]), swap(piece, "row")

    sent = [send(piece) for piece in pieces[:AHEAD]]
    near = [lax.ppermute(piece, "col", mate) for piece in pieces[:AHEAD]]

    done = None
    order = [place, weight, turns[:row_block], turns[row_block:], lane_rows]
    for i, base in enumerate(bases):
        far, other = sent[i]
        if i + AHEAD < len(PARTS):
            far, other, pieces[i + AHEAD], order = lax.optimization_barrier((far, other, pieces[i + AHEAD], order))
            sent.append(send(pieces[i + AHEAD]))
            near.append(lax.ppermute(pieces[i + AHEAD], "col", mate))
        else:
            far, other, order = lax.optimization_barrier((far, other, order))
        if not i:
            place, weight, row_turns, col_turns, lane_rows = order
        else:
            done = order
        rows = [pieces[i], near[i], far, lax.ppermute(far, "col", mate)]
        done = fused(
            base, freq, place, rows, [pieces[i], other], weight,
            row_turns, col_turns, lane_rows, channels, done,
        )
        order = done
    visible, *stored, sums = done
    gain_solution = jnp.transpose(calibrate(stored, sums), (0, 2, 1))
    return (visible.reshape(channels, row_block, 1, 2 * col_block), gain_solution)


def solution(mesh):
    in_specs = (
        P(("row", "col"), "chan", None),
        P("chan"),
        P(),
        P(),
        P(),
        P(),
        P("chan", None),
        P(),
    )
    out_specs = (P("chan", "row", "col", None), P(None, ("row", "col"), "chan"))
    return jax.shard_map(body, mesh=mesh, in_specs=in_specs, out_specs=out_specs, check_vma=False)
```

```python
import functools
import math

import jax
import jax.numpy as jnp
import numpy as np
from jax import lax
from jax.experimental import pallas as pl
from jax.experimental.pallas import tpu as pltpu
from jax.sharding import PartitionSpec as P

ITERS = 3
CHUNKS = 4
PARTS = (4, 5, 5, 5, 3, 2)
AHEAD = 2
HELD, RING = 15, 3
STRIP = 128
MESH = pl.DeviceIdType.MESH


def cosine_coefficients(degree=8):
    nodes = np.cos(np.pi * (np.arange(400) + 0.5) / 400)
    y = 0.125 * (nodes + 1.0)
    fit = np.polynomial.chebyshev.Chebyshev.fit(
        y, np.cos(2.0 * np.pi * np.sqrt(y)), degree, domain=[0.0, 0.25]
    )
    return [float(c) for c in fit.convert(kind=np.polynomial.Polynomial).coef]


COS_COEF = cosine_coefficients()


def cos_turns(turns):
    r = turns - jnp.round(turns)
    y = r * r
    acc = jnp.full_like(y, COS_COEF[-1])
    for c in COS_COEF[-2::-1]:
        acc = acc * y + c
    return acc


def split(x):
    hi = x.astype(jnp.bfloat16)
    lo = (x - hi.astype(jnp.float32)).astype(jnp.bfloat16)
    return hi, lo


def column_sum(x):
    return jnp.sum(x, axis=0, keepdims=True)


NT = (((1,), (1,)), ((), ()))


def correlate_kernel(base, tile, n_rows, n_cols, freq_ref, place_ref, wt_ref, rbase_ref, cbase_ref, lane_ref,
                     *rest):
    rows_refs, cols_refs = rest[:n_rows], rest[n_rows:n_rows + n_cols]
    vis_ref, cre_ref, cim_ref, den_ref, sum_ref, rows_ref, part_ref, steer_ref = rest[-8:]
    samples = rows_ref.shape[1] // 2
    row_block = rows_ref.shape[0]
    col_block = part_ref.shape[0] // 2
    half = lane_ref.shape[1] // 2
    lanes = 2 * half
    freq = freq_ref[base + pl.program_id(0)]
    for j, ref in enumerate(rows_refs):
        size = ref.shape[1]
        at = pl.ds(pl.multiple_of(place_ref[j] * size, size), size) if n_rows > 1 else pl.ds(0, size)
        rows_ref[at, :] = ref[0]
    for j, ref in enumerate(cols_refs):
        size = ref.shape[1]
        start = pl.multiple_of(place_ref[n_rows + j] * size, size) if n_cols > 1 else 0
        scaled = ref[0] * jnp.bfloat16(1.0 / samples)
        part_ref[pl.ds(start, size), :] = scaled
        part_ref[pl.ds(col_block + start, size), :samples] = -scaled[:, samples:]
        part_ref[pl.ds(col_block + start, size), samples:] = scaled[:, :samples]
    offset = lane_ref[0:1, :]
    flux = lane_ref[1:2, :]
    sign = lane_ref[2:3, :]
    col_steer = cos_turns(cbase_ref[...] * freq + offset)
    swapped = pltpu.roll(col_steer, half, 1) * sign
    for j, s in enumerate((col_steer, swapped)):
        hi, lo = split(s)
        at = pl.ds(j * col_block, col_block)
        steer_ref[at, :lanes] = hi
        steer_ref[at, lanes:2 * lanes] = hi
        steer_ref[at, 2 * lanes:] = lo

    def step(i, sums):
        at = pl.ds(pl.multiple_of(i * tile, tile), tile)
        v = lax.dot_general(rows_ref[at, :], part_ref[...], NT, preferred_element_type=jnp.float32)
        vis_ref[0, at, :] = v.astype(jnp.bfloat16)
        hi, lo = split(cos_turns(rbase_ref[at, :] * freq + offset) * flux)
        m = lax.dot_general(
            jnp.concatenate([hi, lo, hi], axis=1), steer_ref[...], NT, preferred_element_type=jnp.float32
        )
        w = wt_ref[at, :]
        vr, vi = v[:, :col_block], v[:, col_block:]
        mr, mi = m[:, :col_block] * w, m[:, col_block:] * w
        cre = vr * mr + vi * mi
        cim = vr * mi - vi * mr
        den = mr * mr + mi * mi
        cre_ref[0, at, :] = cre.astype(jnp.bfloat16)
        cim_ref[0, at, :] = cim.astype(jnp.bfloat16)
        den_ref[0, at, :] = den.astype(jnp.bfloat16)
        return tuple(s + column_sum(x) for s, x in zip(sums, (cre, cim, den)))

    zero = jnp.zeros((1, col_block), jnp.float32)
    sums = lax.fori_loop(0, row_block // tile, step, (zero, zero, zero))
    for j in range(3):
        sum_ref[0, j:j + 1, :] = sums[j]


def correlate(base, freq, place, rows, cols, weight, rbase, cbase, lane_rows, channels, earlier):
    chans, _, width = rows[0].shape
    row_block, col_block = weight.shape
    lanes = lane_rows.shape[1]
    tile = min(256, row_block)

    def whole(a):
        return pl.BlockSpec(a.shape, lambda k: (0,) * a.ndim)

    def slab(*shape):
        return pl.BlockSpec((1,) + shape, lambda k: (k, 0, 0))

    in_specs = [
        pl.BlockSpec(memory_space=pltpu.SMEM),
        pl.BlockSpec(memory_space=pltpu.SMEM),
        whole(weight),
        whole(rbase),
        whole(cbase),
        whole(lane_rows),
    ] + [slab(a.shape[1], width) for a in rows + cols]
    args = [freq, place, weight, rbase, cbase, lane_rows] + rows + cols
    aliases = {}
    if earlier is not None:
        in_specs.append(pl.BlockSpec(memory_space=pl.ANY))
        args.append(earlier)
        aliases = {len(args) - 1: 0}
    stored = jax.ShapeDtypeStruct((chans, row_block, col_block), jnp.bfloat16)
    flops = chans * row_block * 2 * col_block * (2 * width + 6 * lanes)
    return pl.pallas_call(
        functools.partial(correlate_kernel, base, tile, len(rows), len(cols)),
        grid=(chans,),
        in_specs=in_specs,
        out_specs=[
            pl.BlockSpec((1, row_block, 2 * col_block), lambda k: (k + base, 0, 0)),
            slab(row_block, col_block),
            slab(row_block, col_block),
            slab(row_block, col_block),
            slab(3, col_block),
        ],
        out_shape=[
            jax.ShapeDtypeStruct((channels, row_block, 2 * col_block), jnp.bfloat16),
            stored,
            stored,
            stored,
            jax.ShapeDtypeStruct((chans, 3, col_block), jnp.float32),
        ],
        scratch_shapes=[
            pltpu.VMEM((row_block, width), jnp.bfloat16),
            pltpu.VMEM((2 * col_block, width), jnp.bfloat16),
            pltpu.VMEM((2 * col_block, 3 * lanes), jnp.bfloat16),
        ],
        input_output_aliases=aliases,
        compiler_params=pltpu.CompilerParams(vmem_limit_bytes=60 * 2**20),
        cost_estimate=pl.CostEstimate(
            flops=flops, bytes_accessed=chans * row_block * col_block * 14, transcendentals=0
        ),
        name="correlate",
    )(*args)


def gain_kernel(tile, gain_ref, cre_ref, cim_ref, den_ref, sum_ref):
    row_block, col_block = cre_ref.shape[1:]
    total = [jnp.zeros((1, col_block), jnp.float32) for _ in range(3)]
    for i in range(row_block // tile):
        at = pl.ds(i * tile, tile)
        g = jnp.transpose(gain_ref[0, :, i * tile:(i + 1) * tile])
        gr, gi, power = g[:, 0:1], g[:, 1:2], g[:, 2:3]
        cre = cre_ref[0, at, :].astype(jnp.float32)
        cim = cim_ref[0, at, :].astype(jnp.float32)
        den = den_ref[0, at, :].astype(jnp.float32)
        total[0] += column_sum(gr * cre - gi * cim)
        total[1] += column_sum(gr * cim + gi * cre)
        total[2] += column_sum(power * den)
    for j in range(3):
        sum_ref[0, j:j + 1, :] = total[j]


def gain_sums(gain_re, gain_im, cre, cim, den):
    chans, row_block, col_block = cre.shape
    power = gain_re * gain_re + gain_im * gain_im
    gains = jnp.stack([gain_re, gain_im, power] + [jnp.zeros_like(power)] * 5, axis=1)

    def slab(*shape):
        return pl.BlockSpec((1,) + shape, lambda k: (k, 0, 0))

    return pl.pallas_call(
        functools.partial(gain_kernel, min(128, row_block)),
        grid=(chans,),
        in_specs=[slab(8, row_block)] + [slab(row_block, col_block)] * 3,
        out_specs=slab(3, col_block),
        out_shape=jax.ShapeDtypeStruct((chans, 3, col_block), jnp.float32),
        compiler_params=pltpu.CompilerParams(vmem_limit_bytes=60 * 2**20),
        cost_estimate=pl.CostEstimate(
            flops=chans * row_block * col_block * 10,
            bytes_accessed=chans * row_block * col_block * 6,
            transcendentals=0,
        ),
        name="gain_sums",
    )(gains, cre, cim, den)


def swap(x, axis):
    return lax.ppermute(x, axis, [(0, 1), (1, 0)])


def column_blocks(x, n_row):
    if n_row != 2:
        return [jnp.transpose(lax.all_gather(jnp.transpose(x, (1, 0, 2)), "row", axis=0, tiled=True), (1, 0, 2))]
    return [x, swap(x, "row")]


def row_blocks(x, n_col):
    if n_col != 4:
        return [jnp.transpose(lax.all_gather(jnp.transpose(x, (1, 0, 2)), "col", axis=0, tiled=True), (1, 0, 2))]
    far = lax.ppermute(x, "col", [(c, c ^ 2) for c in range(n_col)])
    mate = [(c, c ^ 1) for c in range(n_col)]
    return [x, lax.ppermute(x, "col", mate), far, lax.ppermute(far, "col", mate)]


def own_sums(part, row_id, n_row, sub_block):
    if n_row != 2:
        part = lax.psum(part, "row")
        return lax.dynamic_slice_in_dim(part, row_id * sub_block, sub_block, 2)
    mine = lax.dynamic_slice_in_dim(part, row_id * sub_block, sub_block, 2)
    theirs = lax.dynamic_slice_in_dim(part, (1 - row_id) * sub_block, sub_block, 2)
    return mine + swap(theirs, "row")


def gather_gains(own, col_id, n_col, sub_block):
    if n_col != 4:
        return lax.all_gather(own, "col", axis=2, tiled=True)
    blocks = [own] + [
        lax.ppermute(own, "col", [((c + j) % n_col, c) for c in range(n_col)]) for j in range(1, n_col)
    ]
    twice = jnp.concatenate(blocks + blocks, axis=2)
    return lax.dynamic_slice_in_dim(twice, (n_col - col_id) % n_col * sub_block, n_col * sub_block, 2)


def fused_kernel(base, n_rows, n_cols, freq_ref, place_ref, wt_ref, rbase_ref, cbase_ref, lane_ref, *rest):
    rows_refs, cols_refs = rest[:n_rows], rest[n_rows:n_rows + n_cols]
    vis_ref, cre_ref, cim_ref, den_ref, sum_ref, rows_ref, part_ref, rst_ref, cst_ref = rest[-9:]
    samples = rows_ref.shape[1] // 2
    col_block = part_ref.shape[0] // 2
    half = lane_ref.shape[1] // 2
    lanes = 2 * half
    width = STRIP
    freq = freq_ref[base + pl.program_id(0)]
    for j, ref in enumerate(rows_refs):
        size = ref.shape[1]
        rows_ref[pl.ds(pl.multiple_of(place_ref[j] * size, size), size), :] = ref[0]
    for j, ref in enumerate(cols_refs):
        size = ref.shape[1]
        start = pl.multiple_of(place_ref[n_rows + j] * 2 * size, 2 * size)
        for u in range(size // width):
            scaled = ref[0, u * width:(u + 1) * width, :] * jnp.bfloat16(1.0 / samples)
            at = start + 2 * u * width
            part_ref[pl.ds(at, width), :] = scaled
            part_ref[pl.ds(at + width, width), :samples] = -scaled[:, samples:]
            part_ref[pl.ds(at + width, width), samples:] = scaled[:, :samples]
    offset, flux, sign = lane_ref[0:1, :], lane_ref[1:2, :], lane_ref[2:3, :]
    col_steer = cos_turns(cbase_ref[...] * freq + offset)
    swapped = pltpu.roll(col_steer, half, 1) * sign
    for j, s in enumerate((col_steer, swapped)):
        hi, lo = split(s)
        for u in range(col_block // width):
            at = pl.ds((2 * u + j) * width, width)
            cst_ref[at, :lanes] = hi[u * width:(u + 1) * width]
            cst_ref[at, lanes:] = lo[u * width:(u + 1) * width]
    row_steer = (cos_turns(rbase_ref[...] * freq + offset) * flux).astype(jnp.bfloat16)
    rst_ref[:, :lanes] = row_steer
    rst_ref[:, lanes:] = row_steer
    for u in range(col_block // width):
        strip = slice(2 * u * width, 2 * (u + 1) * width)
        at = slice(u * width, (u + 1) * width)
        v = lax.dot_general(rows_ref[...], part_ref[strip, :], NT, preferred_element_type=jnp.float32)
        m = lax.dot_general(rst_ref[...], cst_ref[strip, :], NT, preferred_element_type=jnp.float32)
        w = wt_ref[:, at]
        vr, vi = v[:, :width], v[:, width:]
        mr, mi = m[:, :width] * w, m[:, width:] * w
        vis_ref[0, :, at] = vr.astype(jnp.bfloat16)
        vis_ref[0, :, col_block + u * width:col_block + (u + 1) * width] = vi.astype(jnp.bfloat16)
        cre = vr * mr + vi * mi
        cim = vr * mi - vi * mr
        den = mr * mr + mi * mi
        for j, (ref, x) in enumerate(((cre_ref, cre), (cim_ref, cim), (den_ref, den))):
            ref[0, :, at] = x.astype(jnp.bfloat16)
            sum_ref[0, j:j + 1, at] = column_sum(x)


def fused(base, freq, place, rows, cols, weight, rbase, cbase, lane_rows, channels, earlier):
    chans, size, width = rows[2].shape
    row_block, col_block = weight.shape
    lanes = lane_rows.shape[1]

    def whole(a):
        return pl.BlockSpec(a.shape, lambda k: (0,) * a.ndim)

    def slab(*shape):
        return pl.BlockSpec((1,) + shape, lambda k: (k, 0, 0))

    def placed(*shape):
        return pl.BlockSpec((1,) + shape, lambda k: (k + base, 0, 0))

    def block(a):
        return slab(size, width) if a.shape[0] == chans else placed(size, width)

    tables = [weight, rbase, cbase, lane_rows]
    in_specs = [pl.BlockSpec(memory_space=pltpu.SMEM)] * 2 + [whole(a) for a in tables]
    in_specs += [block(a) for a in rows + cols]
    args = [freq, place] + tables + rows + cols
    aliases = {}
    for j, array in enumerate(earlier or ()):
        in_specs.append(pl.BlockSpec(memory_space=pl.ANY))
        aliases[len(args)] = j
        args.append(array)
    stored = jax.ShapeDtypeStruct((channels, row_block, col_block), jnp.bfloat16)
    return pl.pallas_call(
        functools.partial(fused_kernel, base, len(rows), len(cols)),
        grid=(chans,),
        in_specs=in_specs,
        out_specs=[placed(row_block, 2 * col_block)] + [placed(row_block, col_block)] * 3 + [placed(3, col_block)],
        out_shape=[jax.ShapeDtypeStruct((channels, row_block, 2 * col_block), jnp.bfloat16)]
        + [stored] * 3
        + [jax.ShapeDtypeStruct((channels, 3, col_block), jnp.float32)],
        scratch_shapes=[
            pltpu.VMEM((row_block, width), jnp.bfloat16),
            pltpu.VMEM((2 * col_block, width), jnp.bfloat16),
            pltpu.VMEM((row_block, 2 * lanes), jnp.bfloat16),
            pltpu.VMEM((2 * col_block, 2 * lanes), jnp.bfloat16),
        ],
        input_output_aliases=aliases,
        compiler_params=pltpu.CompilerParams(vmem_limit_bytes=62 * 2**20),
        cost_estimate=pl.CostEstimate(flops=1, bytes_accessed=1, transcendentals=0),
        name="correlate_fused",
    )(*args)


def calibrate_kernel(counts, held_count, ring, sums_ref, cre_hbm, cim_hbm, den_hbm, out_ref, cre, cim, den, lhs,
                     part_a, part_b, landed_a, landed_b, gain_a, gain_b, load_sem, send_sem, recv_sem):
    held = (cre, cim, den)
    parts, landings, gains = (part_a, part_b), (landed_a, landed_b), (gain_a, gain_b)
    firsts = (0, counts[0])
    total = sum(counts)
    turning = total - held_count
    sub = part_a.shape[3]
    r, c = lax.axis_index("row"), lax.axis_index("col")
    cols = [c, c + 1 - 2 * (c % 2), (c + 2) % 4, 3 - c]
    peers = [(d, j) for d in range(2) for j in range(4) if d or j]
    spots = {(d, j): ((1 - r) if d else r, cols[j]) for d, j in peers}
    barrier = pltpu.get_barrier_semaphore()
    for peer in peers:
        row, col = spots[peer]
        pl.semaphore_signal(barrier, inc=1, device_id={"row": row, "col": col}, device_id_type=MESH)

    def loads(k, slot):
        return [
            pltpu.make_async_copy(src.at[k], dst.at[slot], load_sem.at[slot, j])
            for j, (src, dst) in enumerate(zip((cre_hbm, cim_hbm, den_hbm), held))
        ]

    def fetch(k, carry):
        for copy in loads(k, k):
            copy.start()
        return carry

    lax.fori_loop(0, held_count + ring, fetch, 0)
    def fill(side):
        for j in range(3):
            for h in range(2):
                for k in range(counts[side]):
                    parts[side][h, j, k:k + 1, :] = sums_ref[firsts[side] + k, j:j + 1, h * sub:(h + 1) * sub]

    def fits(k, slot, part, at):
        matrix = lhs[k].astype(jnp.bfloat16)
        a, b, d = (jnp.dot(matrix, m[slot], preferred_element_type=jnp.float32) for m in held)
        rows = (
            a[0:1] + a[1:2] - b[2:3] - b[3:4],
            b[0:1] + b[1:2] + a[2:3] + a[3:4],
            d[4:5] + d[5:6],
        )
        for j, row in enumerate(rows):
            for h in range(2):
                part[h, j, pl.ds(at, 1), :] = row[:, h * sub:(h + 1) * sub]

    def refit(side, iteration):
        first, last = firsts[side], firsts[side] + counts[side]

        def resident(k, carry):
            if iteration == 1:
                for copy in loads(k, k):
                    copy.wait()
            fits(k, k, parts[side], k - first)
            return carry

        def turned(k, carry):
            slot = held_count + (k - held_count) % ring
            for copy in loads(k, slot):
                copy.wait()
            fits(k, slot, parts[side], k - first)
            following = held_count + (k - held_count + ring) % turning

            def start():
                for copy in loads(following, slot):
                    copy.start()

            if iteration == 1:
                start()
            else:
                pl.when(k + ring < total)(start)
            return carry

        split_at = min(max(held_count, first), last)
        if first < split_at:
            lax.fori_loop(first, split_at, resident, 0)
        if split_at < last:
            lax.fori_loop(split_at, last, turned, 0)

    def send(side, iteration):
        part, landed = parts[side], landings[side]
        copies = []
        for d, j in [(1, 0)] if iteration + 1 == ITERS else peers:
            row, col = spots[d, j]
            copies.append(
                pltpu.make_async_remote_copy(
                    src_ref=part.at[row],
                    dst_ref=landed.at[iteration, r, c],
                    send_sem=send_sem.at[side, iteration, 4 * d + j],
                    recv_sem=recv_sem.at[side, iteration, 4 * d + j],
                    device_id={"row": row, "col": col},
                    device_id_type=MESH,
                )
            )
        for copy in copies:
            copy.start()
        landed[iteration, r, c] = part[r]
        return copies

    def update(side, iteration, block):
        sums = landings[side][iteration, 0, block] + landings[side][iteration, 1, block]
        total = sums[2] + 1e-06
        if iteration:
            re, im = gains[side][block, 0], gains[side][block, 1]
        else:
            re, im = jnp.ones_like(total), jnp.zeros_like(total)
        return (re + sums[0] / total) * 0.5, (im + sums[1] / total) * 0.5

    def advance(side, iteration):
        for b in range(4):
            re, im = update(side, iteration, b)
            gains[side][b, 0], gains[side][b, 1] = re, im
            rows = []
            for x in (re, im, re * re + im * im):
                hi = x.astype(jnp.bfloat16).astype(jnp.float32)
                rows += [hi, x - hi]
            for k in range(counts[side]):
                for j, x in enumerate(rows):
                    lhs[firsts[side] + k, j:j + 1, b * sub:(b + 1) * sub] = x[k:k + 1]

    fill(0)
    pl.semaphore_wait(barrier, len(peers))
    pending = [send(0, 0)]
    fill(1)
    pending.append(send(1, 0))
    lhs[...] = jnp.zeros_like(lhs)
    for iteration in range(1, ITERS):
        for side in range(2):
            for copy in pending[side]:
                copy.wait()
            advance(side, iteration - 1)
            refit(side, iteration)
            pending[side] = send(side, iteration)
    for side in range(2):
        for copy in pending[side]:
            copy.wait()
        re, im = update(side, ITERS - 1, c)
        at = slice(firsts[side], firsts[side] + counts[side])
        out_ref[0, at, :], out_ref[1, at, :] = re, im


def calibrate(stored, sums):
    chans, row_block, col_block = stored[0].shape
    counts = (chans * 2 // 3, chans - chans * 2 // 3)
    sub = col_block // 2
    held = pltpu.VMEM((HELD + RING, row_block, col_block), jnp.bfloat16)
    in_vmem = pl.BlockSpec(memory_space=pltpu.VMEM)
    return pl.pallas_call(
        functools.partial(calibrate_kernel, counts, HELD, RING),
        in_specs=[in_vmem] + [pl.BlockSpec(memory_space=pl.ANY)] * 3,
        out_specs=in_vmem,
        out_shape=jax.ShapeDtypeStruct((2, chans, sub), jnp.float32),
        scratch_shapes=[held, held, held, pltpu.VMEM((chans, 16, row_block), jnp.float32)]
        + [pltpu.VMEM((2, 3, n, sub), jnp.float32) for n in counts]
        + [pltpu.VMEM((ITERS, 2, 4, 3, n, sub), jnp.float32) for n in counts]
        + [pltpu.VMEM((4, 2, n, sub), jnp.float32) for n in counts]
        + [
            pltpu.SemaphoreType.DMA((HELD + RING, 3)),
            pltpu.SemaphoreType.DMA((2, ITERS, 8)),
            pltpu.SemaphoreType.DMA((2, ITERS, 8)),
        ],
        compiler_params=pltpu.CompilerParams(
            collective_id=0, has_side_effects=True, vmem_limit_bytes=62 * 2**20
        ),
        cost_estimate=pl.CostEstimate(
            flops=chans * row_block * col_block * 40,
            bytes_accessed=chans * row_block * col_block * 8,
            transcendentals=0,
        ),
        name="calibrate",
    )(sums, *stored)


def body(
    voltage,
    channel_frequency_offset,
    input_antenna_lookup,
    antenna_positions,
    catalogue_direction,
    catalogue_flux,
    sky_source_index,
    baseline_tile_flagged,
):
    highest = lax.Precision.HIGHEST
    n_row = lax.axis_size("row")
    n_col = lax.axis_size("col")
    sub_block, channels, width = voltage.shape
    row_block = sub_block * n_col
    col_block = sub_block * n_row
    total = row_block * n_row
    row_id = lax.axis_index("row")
    col_id = lax.axis_index("col")

    chunk = channels // CHUNKS if channels % CHUNKS == 0 else channels
    spots = [col_id ^ j for j in range(4)] if n_col == 4 else [0 * col_id]
    spots += [row_id, 1 - row_id] if n_row == 2 else [0 * row_id]
    place = jnp.stack(spots).astype(jnp.int32)

    row_ids = row_id * row_block + jnp.arange(row_block, dtype=jnp.int32)
    slots = jnp.arange(col_block, dtype=jnp.int32)
    col_ids = slots // sub_block * row_block + col_id * sub_block + slots % sub_block
    tiles = baseline_tile_flagged.shape[0]
    tile_width = total // tiles
    kept = 1.0 - jnp.maximum(baseline_tile_flagged, baseline_tile_flagged.T).astype(jnp.float32)
    tile_ids = jnp.arange(tiles, dtype=jnp.int32)
    row_pick = (row_ids[:, None] // tile_width == tile_ids).astype(jnp.float32)
    col_pick = (col_ids[:, None] // tile_width == tile_ids).astype(jnp.float32)
    weight = jnp.dot(jnp.dot(row_pick, kept), col_pick.T)

    row_antennas = lax.dynamic_slice_in_dim(input_antenna_lookup, row_id * row_block, row_block)
    col_antennas = lax.dynamic_slice_in_dim(
        input_antenna_lookup.reshape(n_row, n_col, sub_block), col_id, 1, 1
    ).reshape(col_block)
    antennas = jnp.concatenate([row_antennas, col_antennas])
    picked = (antennas[:, None] == jnp.arange(total, dtype=jnp.int32)).astype(jnp.float32)
    where = jnp.dot(picked, antenna_positions.T, precision=highest)
    sources = sky_source_index[0]
    catalogue = jnp.concatenate([catalogue_direction, catalogue_flux[None]], axis=0)
    chosen = (sources[:, None] == jnp.arange(catalogue.shape[1], dtype=jnp.int32)).astype(jnp.float32)
    sky = lax.dot_general(catalogue, chosen, (((1,), (1,)), ((), ())), precision=highest)
    twice = jnp.concatenate([sky, sky], axis=1)
    turns = where[:, 0:1] * twice[0:1] + where[:, 1:2] * twice[1:2]
    n_src = sources.shape[0]
    ones = jnp.ones((n_src,), jnp.float32)
    lane_rows = jnp.stack(
        [jnp.concatenate([0.0 * ones, 0.25 * ones]), twice[2], jnp.concatenate([-ones, ones])]
        + [jnp.zeros((2 * n_src,), jnp.float32)] * 5
    )

    if n_row == 2 and n_col == 4 and channels == sum(PARTS) and sub_block % STRIP == 0 and 2 * n_src == 128:
        return pipelined(voltage, channel_frequency_offset, place, weight, turns, lane_rows)

    visible = None
    finals = []
    done = []
    for base in range(0, channels, chunk):
        piece = jnp.transpose(voltage[:, base:base + chunk, :], (1, 0, 2))
        if len(done) >= 2:
            piece, done[-2][3] = lax.optimization_barrier((piece, done[-2][3]))
        rows, cols = row_blocks(piece, n_col), column_blocks(piece, n_row)
        visible, *kept_sums = correlate(
            base, channel_frequency_offset, place, rows, cols, weight,
            turns[:row_block], turns[row_block:], lane_rows, channels, visible,
        )
        done.append(kept_sums)
    for cre, cim, den, part in done:
        own = None
        for iteration in range(ITERS):
            if iteration:
                gains = gather_gains(own, col_id, n_col, sub_block)
                part = gain_sums(gains[:, 0], gains[:, 1], cre, cim, den)
            sums = own_sums(part, row_id, n_row, sub_block)
            if own is None:
                own = jnp.concatenate([jnp.ones_like(sums[:, :1]), jnp.zeros_like(sums[:, :1])], axis=1)
            own = (own + sums[:, :2] / (sums[:, 2:3] + 1e-06)) * 0.5
        finals.append(own)
    gain_solution = jnp.transpose(jnp.concatenate(finals, axis=0), (1, 2, 0))
    return (visible.reshape(channels, row_block, 1, 2 * col_block), gain_solution)


def pipelined(voltage, freq, place, weight, turns, lane_rows):
    sub_block, channels, width = voltage.shape
    row_block, col_block = weight.shape
    mate = [(c, c ^ 1) for c in range(4)]
    bases = [sum(PARTS[:i]) for i in range(len(PARTS))]
    pieces = [jnp.transpose(voltage[:, b:b + n, :], (1, 0, 2)) for b, n in zip(bases, PARTS)]

    def send(piece):
        return lax.ppermute(piece, "col", [(c, c ^ 2) for c in range(4)]), swap(piece, "row")

    sent = [send(piece) for piece in pieces[:AHEAD]]
    near = [lax.ppermute(piece, "col", mate) for piece in pieces[:AHEAD]]

    done = None
    order = [place, weight, turns[:row_block], turns[row_block:], lane_rows]
    for i, base in enumerate(bases):
        far, other = sent[i]
        if i + AHEAD < len(PARTS):
            far, other, pieces[i + AHEAD], order = lax.optimization_barrier((far, other, pieces[i + AHEAD], order))
            sent.append(send(pieces[i + AHEAD]))
            near.append(lax.ppermute(pieces[i + AHEAD], "col", mate))
        else:
            far, other, order = lax.optimization_barrier((far, other, order))
        if not i:
            place, weight, row_turns, col_turns, lane_rows = order
        else:
            done = order
        rows = [pieces[i], near[i], far, lax.ppermute(far, "col", mate)]
        done = fused(
            base, freq, place, rows, [pieces[i], other], weight,
            row_turns, col_turns, lane_rows, channels, done,
        )
        order = done
    visible, *stored, sums = done
    gain_solution = jnp.transpose(calibrate(stored, sums), (0, 2, 1))
    return (visible.reshape(channels, row_block, 1, 2 * col_block), gain_solution)


def solution(mesh):
    in_specs = (
        P(("row", "col"), "chan", None),
        P("chan"),
        P(),
        P(),
        P(),
        P(),
        P("chan", None),
        P(),
    )
    out_specs = (P("chan", "row", "col", None), P(None, ("row", "col"), "chan"))
    return jax.shard_map(body, mesh=mesh, in_specs=in_specs, out_specs=out_specs, check_vma=False)
```
